32 devices in a mesh: dp: 16 (over z, x, core), seq: 2 (over y).
Axes of the slice: x: 2, y: 2, z: 4, core: 2. Of those that a mesh axis runs over, the one named last changes fastest.
Arguments:
- images: bfloat16 [32, 592, 1024], P('dp', 'seq'), may hold values from -6 to 6
- cotangent: bfloat16 [32, 592, 1024], P('dp', 'seq'), may hold values from -6 to 6
- w_qkv: float32 [1024, 3072], P('dp', 'seq'), may hold values from -0.1875 to 0.1875
- w_out: float32 [1024, 1024], P('dp', 'seq'), may hold values from -1 to 1
- w_up: float32 [1024, 4096], P('dp', 'seq'), may hold values from -0.1875 to 0.1875
- w_down: float32 [4096, 1024], P('dp', 'seq'), may hold values from -0.09375 to 0.09375
- gains: float32 [2, 1024], P(None, ('dp', 'seq')), may hold values from 0.5 to 1.5
- biases: float32 [10, 1024], P(None, ('dp', 'seq')), may hold values from -3 to 3
- first_qkv: float32 [1024, 3072], P('dp', 'seq'), may hold values from -120 to 120
- first_out: float32 [1024, 1024], P('dp', 'seq'), may hold values from -120 to 120
- first_up: float32 [1024, 4096], P('dp', 'seq'), may hold values from -120 to 120
- first_down: float32 [4096, 1024], P('dp', 'seq'), may hold values from -120 to 120
- first_gains: float32 [2, 1024], P(None, ('dp', 'seq')), may hold values from -120 to 120
- first_biases: float32 [10, 1024], P(None, ('dp', 'seq')), may hold values from -120 to 120
- second_qkv: float32 [1024, 3072], P('dp', 'seq'), may hold values from 100 to 10000
- second_out: float32 [1024, 1024], P('dp', 'seq'), may hold values from 100 to 10000
- second_up: float32 [1024, 4096], P('dp', 'seq'), may hold values from 100 to 10000
- second_down: float32 [4096, 1024], P('dp', 'seq'), may hold values from 100 to 10000
- second_gains: float32 [2, 1024], P(None, ('dp', 'seq')), may hold values from 100 to 10000
- second_biases: float32 [10, 1024], P(None, ('dp', 'seq')), may hold values from 100 to 10000
Outputs:
- out_images: bfloat16 [32, 592, 1024], P('dp', 'seq')
- grad_images: bfloat16 [32, 592, 1024], P('dp', 'seq')
- grad_qkv: float32 [1024, 3072], P('dp', 'seq')
- grad_out: float32 [1024, 1024], P('dp', 'seq')
- grad_up: float32 [1024, 4096], P('dp', 'seq')
- grad_down: float32 [4096, 1024], P('dp', 'seq')
- grad_gains: float32 [2, 1024], P(None, ('dp', 'seq'))
- grad_biases: float32 [10, 1024], P(None, ('dp', 'seq'))
- new_qkv: float32 [1024, 3072], P('dp', 'seq')
- new_out: float32 [1024, 1024], P('dp', 'seq')
- new_up: float32 [1024, 4096], P('dp', 'seq')
- new_down: float32 [4096, 1024], P('dp', 'seq')
- new_gains: float32 [2, 1024], P(None, ('dp', 'seq'))
- new_biases: float32 [10, 1024], P(None, ('dp', 'seq'))
- new_first_qkv: float32 [1024, 3072], P('dp', 'seq')
- new_first_out: float32 [1024, 1024], P('dp', 'seq')
- new_first_up: float32 [1024, 4096], P('dp', 'seq')
- new_first_down: float32 [4096, 1024], P('dp', 'seq')
- new_first_gains: float32 [2, 1024], P(None, ('dp', 'seq'))
- new_first_biases: float32 [10, 1024], P(None, ('dp', 'seq'))
- new_second_qkv: float32 [1024, 3072], P('dp', 'seq')
- new_second_out: float32 [1024, 1024], P('dp', 'seq')
- new_second_up: float32 [1024, 4096], P('dp', 'seq')
- new_second_down: float32 [4096, 1024], P('dp', 'seq')
- new_second_gains: float32 [2, 1024], P(None, ('dp', 'seq'))
- new_second_biases: float32 [10, 1024], P(None, ('dp', 'seq'))
The draws below stay inside these ranges and needn't reach their ends.
All inputs are finite; a program needn't handle non-finite values.
Results may differ from the reference program's by a relative error of at most 0.028.
Values may be sent and summed in bfloat16 or wider, within the bound.
A program may use at most 256 MiB of HBM per device.

```python
import math
import jax
import jax.numpy as jnp
from jax import lax

D = 1024
HEAD_DIM = 64
FF = 4096
PATCH_TOK = 577
STEP = 5
SEQ_PAD = 592
IMAGES = 32


def steps_of(key, shape, shards, least, high):
    factor_of, own = 1.0, jax.random.fold_in(key, 6)
    for position, parts in shards:
        heights = jnp.exp(jax.random.uniform(jax.random.fold_in(own, position), (parts,), jnp.float32, least / len(shards), high / len(shards)))
        factor_of = factor_of * jnp.repeat(heights, shape[position] // parts).reshape([-1 if axis == position else 1 for axis in range(len(shape))])
    return factor_of


def normal_values(own_key, shape, deviation, most, split=(), kind=jnp.bfloat16):
    entries = deviation * jax.random.normal(own_key, shape, jnp.float32)
    if split:
        entries = entries * steps_of(own_key, shape, split, -0.22, 0.18)
    return jnp.clip(entries, -most, most).astype(kind)


def setup_inputs(seed: int = 0) -> dict:
    splits = jax.random.split(jax.random.key(seed), 21)
    return {
        "images": normal_values(splits[0], (IMAGES, SEQ_PAD, D), 1.0, 6.0, ((0, 16), (1, 2))),
        "cotangent": normal_values(splits[1], (IMAGES, SEQ_PAD, D), 1.0, 6.0, ((0, 16), (1, 2))),
        "w_qkv": normal_values(splits[2], (D, 3 * D), D ** -0.5, 0.1875, ((0, 16), (1, 2)), jnp.float32),
        "w_out": normal_values(splits[3], (D, D), (D // 24) ** -0.5, 1.0, ((0, 16), (1, 2)), jnp.float32),
        "w_up": normal_values(splits[4], (D, FF), D ** -0.5, 0.1875, ((0, 16), (1, 2)), jnp.float32),
        "w_down": normal_values(splits[5], (FF, D), FF ** -0.5, 0.09375, ((0, 16), (1, 2)), jnp.float32),
        "gains": jnp.clip(1.0 + 0.1 * jax.random.normal(splits[6], (2, D), jnp.float32), 0.5, 1.5),
        "biases": normal_values(splits[7], (10, D), 0.5, 3.0, ((1, 32),), jnp.float32),
        "first_qkv": normal_values(splits[8], (D, 3 * D), 20.0, 120.0, ((0, 16), (1, 2)), jnp.float32),
        "first_out": normal_values(splits[9], (D, D), 20.0, 120.0, ((0, 16), (1, 2)), jnp.float32),
        "first_up": normal_values(splits[10], (D, FF), 20.0, 120.0, ((0, 16), (1, 2)), jnp.float32),
        "first_down": normal_values(splits[11], (FF, D), 20.0, 120.0, ((0, 16), (1, 2)), jnp.float32),
        "first_gains": normal_values(splits[12], (2, D), 20.0, 120.0, ((1, 32),), jnp.float32),
        "first_biases": normal_values(splits[13], (10, D), 20.0, 120.0, ((1, 32),), jnp.float32),
        "second_qkv": jnp.clip(jnp.exp(math.log(10000.0) - 4.6051702 * jax.random.uniform(splits[14], (D, 3 * D), jnp.float32) ** steps_of(splits[14], (D, 3 * D), ((0, 16), (1, 2)), -0.2, 0.2)), 100.0, 10000.0),
        "second_out": jnp.clip(jnp.exp(math.log(10000.0) - 4.6051702 * jax.random.uniform(splits[15], (D, D), jnp.float32) ** steps_of(splits[15], (D, D), ((0, 16), (1, 2)), -0.2, 0.2)), 100.0, 10000.0),
        "second_up": jnp.clip(jnp.exp(math.log(10000.0) - 4.6051702 * jax.random.uniform(splits[16], (D, FF), jnp.float32) ** steps_of(splits[16], (D, FF), ((0, 16), (1, 2)), -0.2, 0.2)), 100.0, 10000.0),
        "second_down": jnp.clip(jnp.exp(math.log(10000.0) - 4.6051702 * jax.random.uniform(splits[17], (FF, D), jnp.float32) ** steps_of(splits[17], (FF, D), ((0, 16), (1, 2)), -0.2, 0.2)), 100.0, 10000.0),
        "second_gains": jnp.clip(jnp.exp(math.log(10000.0) - 4.6051702 * jax.random.uniform(splits[18], (2, D), jnp.float32) ** steps_of(splits[18], (2, D), ((1, 32),), -0.2, 0.2)), 100.0, 10000.0),
        "second_biases": jnp.clip(jnp.exp(math.log(10000.0) - 4.6051702 * jax.random.uniform(splits[19], (10, D), jnp.float32) ** steps_of(splits[19], (10, D), ((1, 32),), -0.2, 0.2)), 100.0, 10000.0),
    }


def rounded(values):
    return lax.optimization_barrier(values.astype(jnp.bfloat16)).astype(jnp.float32)

def normalize(rows):
    center = rows - lax.optimization_barrier(jnp.mean(rows, axis=-1, keepdims=True))
    inverse = lax.rsqrt(lax.optimization_barrier(jnp.mean(center * center, axis=-1, keepdims=True)) + 1e-06)
    return (center * inverse, inverse)

def norm_back(grad_out, normed, inverse, gain):
    scaled = grad_out * gain
    return inverse * (scaled - lax.optimization_barrier(jnp.mean(scaled, axis=-1, keepdims=True)) - normed * lax.optimization_barrier(jnp.mean(scaled * normed, axis=-1, keepdims=True)))

def gelu_value(pre):
    return pre * 0.5 * (1.0 + lax.erf(pre * 0.7071067811865476))

def gelu_slope(pre):
    return 0.5 * (1.0 + lax.erf(pre * 0.7071067811865476)) + pre * jnp.exp(-0.5 * pre * pre) * 0.3989422804014327

def layer_pass(image, grad_in, kernels, live):
    w_qkv, w_out, w_up, w_down, gains, biases = kernels
    width = image.shape[-1]
    heads = width // HEAD_DIM
    scale = HEAD_DIM ** (-0.5)
    gain = gains.astype(jnp.float32)
    bias = biases.astype(jnp.float32)
    rows = image.astype(jnp.float32)
    normed_a, inverse_a = normalize(rows)
    hidden_a = (normed_a * gain[0] + bias[0]).astype(jnp.bfloat16)
    mixed = jnp.dot(hidden_a, w_qkv, preferred_element_type=jnp.float32)
    queries = (mixed[:, :width] + bias[1]).astype(jnp.bfloat16)
    keys = mixed[:, width:2 * width].astype(jnp.bfloat16)
    values = (mixed[:, 2 * width:] + bias[2]).astype(jnp.bfloat16)
    query_heads = queries.astype(jnp.float32).reshape(-1, heads, HEAD_DIM)
    key_heads = keys.astype(jnp.float32).reshape(-1, heads, HEAD_DIM)
    value_heads = values.astype(jnp.float32).reshape(-1, heads, HEAD_DIM)
    scores = jnp.einsum('chd,shd->hcs', query_heads, key_heads) * scale
    scores = jnp.where(live[None, None, :], scores, -1e+30)
    top = lax.optimization_barrier(jnp.max(scores, axis=-1, keepdims=True))
    lse = top + jnp.log(lax.optimization_barrier(jnp.sum(jnp.exp(scores - top), axis=-1, keepdims=True)))
    probs = jnp.exp(scores - lse)
    probs_b = rounded(probs)
    context = jnp.einsum('hcs,shd->chd', probs_b, value_heads).reshape(-1, width).astype(jnp.bfloat16)
    resid = rows + jnp.dot(context, w_out, preferred_element_type=jnp.float32) + bias[3]
    normed_b, inverse_b = normalize(resid)
    hidden_b = (normed_b * gain[1] + bias[4]).astype(jnp.bfloat16)
    pre = jnp.dot(hidden_b, w_up, preferred_element_type=jnp.float32) + bias[6:].reshape(-1)
    active = gelu_value(pre).astype(jnp.bfloat16)
    output = (resid + jnp.dot(active, w_down, preferred_element_type=jnp.float32) + bias[5]).astype(jnp.bfloat16)
    grad_y = grad_in.astype(jnp.float32) * live[:, None].astype(jnp.float32)
    grad_yb = grad_y.astype(jnp.bfloat16)
    g_down = jnp.dot(active.T, grad_yb, preferred_element_type=jnp.float32)
    grad_pre = jnp.dot(grad_yb, w_down.T, preferred_element_type=jnp.float32) * gelu_slope(pre)
    grad_preb = grad_pre.astype(jnp.bfloat16)
    g_up = jnp.dot(hidden_b.T, grad_preb, preferred_element_type=jnp.float32)
    grad_hb = jnp.dot(grad_preb, w_up.T, preferred_element_type=jnp.float32)
    grad_resid = grad_y + norm_back(grad_hb, normed_b, inverse_b, gain[1])
    grad_rb = grad_resid.astype(jnp.bfloat16)
    g_outw = jnp.dot(context.T, grad_rb, preferred_element_type=jnp.float32)
    grad_ctx = rounded(jnp.dot(grad_rb, w_out.T, preferred_element_type=jnp.float32)).reshape(-1, heads, HEAD_DIM)
    grad_probs = jnp.einsum('chd,shd->hcs', grad_ctx, value_heads)
    grad_vals = jnp.einsum('hcs,chd->shd', probs_b, grad_ctx).reshape(-1, width)
    delta = lax.optimization_barrier(jnp.sum(probs * grad_probs, axis=-1, keepdims=True))
    grad_scores = rounded(probs * (grad_probs - delta) * scale)
    grad_q = jnp.einsum('hcs,shd->chd', grad_scores, key_heads).reshape(-1, width)
    grad_k = jnp.einsum('hcs,chd->shd', grad_scores, query_heads).reshape(-1, width)
    grad_mixed = jnp.concatenate([grad_q, grad_k, grad_vals], axis=-1).astype(jnp.bfloat16)
    g_qkv = jnp.dot(hidden_a.T, grad_mixed, preferred_element_type=jnp.float32)
    grad_ha = jnp.dot(grad_mixed, w_qkv.T, preferred_element_type=jnp.float32)
    grad_rows = grad_resid + norm_back(grad_ha, normed_a, inverse_a, gain[0])
    g_gains = jnp.stack([lax.optimization_barrier(jnp.sum(grad_ha * normed_a, axis=0)), lax.optimization_barrier(jnp.sum(grad_hb * normed_b, axis=0))])
    g_biases = jnp.concatenate([jnp.stack([lax.optimization_barrier(jnp.sum(grad_ha, axis=0)), lax.optimization_barrier(jnp.sum(grad_q, axis=0)), lax.optimization_barrier(jnp.sum(grad_vals, axis=0)), lax.optimization_barrier(jnp.sum(grad_resid, axis=0)), lax.optimization_barrier(jnp.sum(grad_hb, axis=0)), lax.optimization_barrier(jnp.sum(grad_y, axis=0))]), lax.optimization_barrier(jnp.sum(grad_pre, axis=0)).reshape(-1, width)], axis=0)
    return ((output, grad_rows.astype(jnp.bfloat16)), (g_qkv, g_outw, g_up, g_down, g_gains, g_biases))

def adamw(param, grad, first, second):
    first_new = 0.9 * first + 0.1 * grad
    second_new = 0.95 * second + 0.05 * grad * grad
    step_size = first_new / (1.0 - 0.9 ** STEP) / (jnp.sqrt(second_new / (1.0 - 0.95 ** STEP)) + 1e-08)
    return (param - 0.004 * (step_size + 0.05 * param), first_new, second_new)

def reference(images, cotangent, w_qkv, w_out, w_up, w_down, gains, biases, first_qkv, first_out, first_up, first_down, first_gains, first_biases, second_qkv, second_out, second_up, second_down, second_gains, second_biases):
    params = (w_qkv, w_out, w_up, w_down, gains, biases)
    firsts = (first_qkv, first_out, first_up, first_down, first_gains, first_biases)
    seconds = (second_qkv, second_out, second_up, second_down, second_gains, second_biases)
    kernels = tuple((param.astype(jnp.bfloat16) for param in params))
    live = jnp.arange(SEQ_PAD) < PATCH_TOK

    def per_image(carry, item):
        outputs, grads = layer_pass(item[0], item[1], kernels, live)
        return (tuple((total + grad for total, grad in zip(carry, grads))), outputs)
    start = tuple((jnp.zeros(param.shape, jnp.float32) for param in params))
    totals, (out_images, grad_images) = lax.scan(per_image, start, (images, cotangent))
    updated = [adamw(param, grad, first, second) for param, grad, first, second in zip(params, totals, firsts, seconds)]
    news = tuple((entry[0] for entry in updated))
    new_firsts = tuple((entry[1] for entry in updated))
    new_seconds = tuple((entry[2] for entry in updated))
    return (out_images, grad_images, totals[0], totals[1], totals[2], totals[3], totals[4], totals[5], news[0], news[1], news[2], news[3], news[4], news[5], new_firsts[0], new_firsts[1], new_firsts[2], new_firsts[3], new_firsts[4], new_firsts[5], new_seconds[0], new_seconds[1], new_seconds[2], new_seconds[3], new_seconds[4], new_seconds[5])
```

```python
import jax
import jax.numpy as jnp
from jax import lax
from jax.experimental import pallas as pl
from jax.experimental.pallas import tpu as pltpu
from jax.sharding import PartitionSpec as P

HEAD_DIM = 64
PATCH_TOK = 577
STEP = 5


def normalize(rows):
    center = rows - jnp.mean(rows, axis=-1, keepdims=True)
    inverse = lax.rsqrt(jnp.mean(center * center, axis=-1, keepdims=True) + 1e-06)
    return (center * inverse, inverse)


def norm_back(grad_out, normed, inverse, gain):
    scaled = grad_out * gain
    return inverse * (
        scaled
        - jnp.mean(scaled, axis=-1, keepdims=True)
        - normed * jnp.mean(scaled * normed, axis=-1, keepdims=True)
    )


def gelu_value(pre):
    return pre * 0.5 * (1.0 + lax.erf(pre * 0.7071067811865476))


def gelu_slope(pre):
    return (
        0.5 * (1.0 + lax.erf(pre * 0.7071067811865476))
        + pre * jnp.exp(-0.5 * pre * pre) * 0.3989422804014327
    )


def adamw(param, grad, first, second):
    first_new = 0.9 * first + 0.1 * grad
    second_new = 0.95 * second + 0.05 * grad * grad
    step_size = first_new / (1.0 - 0.9**STEP) / (jnp.sqrt(second_new / (1.0 - 0.95**STEP)) + 1e-08)
    return (param - 0.004 * (step_size + 0.05 * param), first_new, second_new)


LANES = 128
NT = (((1,), (1,)), ((), ()))
NN = (((1,), (0,)), ((), ()))
TN = (((0,), (0,)), ((), ()))


def dot(a, b, dims):
    return lax.dot_general(a, b, dims, preferred_element_type=jnp.float32)


def head_masks(rows, dtype):
    lane = lax.broadcasted_iota(jnp.int32, (rows, LANES), 1)
    return [
        ((lane >= h * HEAD_DIM) & (lane < (h + 1) * HEAD_DIM)) for h in range(LANES // HEAD_DIM)
    ]


def attend_kernel(q_ref, k_ref, v_ref, live_ref, ctx_ref):
    q, k, v = q_ref[0], k_ref[0], v_ref[0]
    live = live_ref[...] > 0.5
    total = jnp.zeros(q.shape, jnp.float32)
    zero = jnp.zeros_like(q)
    for mask in head_masks(q.shape[0], q.dtype):
        scores = dot(jnp.where(mask, q, zero), k, NT) * (HEAD_DIM**-0.5)
        scores = jnp.where(live, scores, -1e30)
        top = jnp.max(scores, axis=-1, keepdims=True)
        weights = jnp.exp(scores - top)
        denom = jnp.sum(weights, axis=-1, keepdims=True)
        probs = (weights * (1.0 / denom)).astype(jnp.bfloat16)
        total = jnp.where(mask, dot(probs, v, NN), total)
    ctx_ref[0] = total.astype(jnp.bfloat16)


def attend_back_kernel(q_ref, k_ref, v_ref, g_ref, live_ref, dq_ref, dk_ref, dv_ref):
    q, k, v, g = q_ref[0], k_ref[0], v_ref[0], g_ref[0]
    live = live_ref[...] > 0.5
    zero_q = jnp.zeros_like(q)
    zero_k = jnp.zeros_like(k)
    dq = jnp.zeros(q.shape, jnp.float32)
    dk = jnp.zeros(k.shape, jnp.float32)
    dv = jnp.zeros(k.shape, jnp.float32)
    masks_q = head_masks(q.shape[0], q.dtype)
    masks_k = head_masks(k.shape[0], k.dtype)
    for mask, mask_k in zip(masks_q, masks_k):
        q_h = jnp.where(mask, q, zero_q)
        g_h = jnp.where(mask, g, zero_q)
        k_h = jnp.where(mask_k, k, zero_k)
        scores = dot(k, q_h, NT) * (HEAD_DIM**-0.5)
        scores = jnp.where(live, scores, -1e30)
        top = jnp.max(scores, axis=0, keepdims=True)
        weights = jnp.exp(scores - top)
        denom = jnp.sum(weights, axis=0, keepdims=True)
        probs = weights * (1.0 / denom)
        grad_probs = dot(v, g_h, NT)
        delta = jnp.sum(probs * grad_probs, axis=0, keepdims=True)
        grad_scores = (probs * (grad_probs - delta) * (HEAD_DIM**-0.5)).astype(jnp.bfloat16)
        dv = dv + dot(probs.astype(jnp.bfloat16), g_h, NN)
        dk = dk + dot(grad_scores, q_h, NN)
        dq = dq + dot(grad_scores, k_h, TN)
    dq_ref[0] = dq
    dk_ref[0] = dk.astype(dk_ref.dtype)
    dv_ref[0] = dv.astype(dv_ref.dtype)


def attend(queries, keys, values, live):
    count, rows, width = queries.shape
    length = keys.shape[1]
    q_spec = pl.BlockSpec((1, rows, LANES), lambda i, h: (i, 0, h))
    k_spec = pl.BlockSpec((1, length, LANES), lambda i, h: (i, 0, h))
    pairs = count * rows * length * width
    return pl.pallas_call(
        attend_kernel,
        grid=(count, width // LANES),
        in_specs=[q_spec, k_spec, k_spec, pl.BlockSpec((1, length), lambda i, h: (0, 0))],
        out_specs=q_spec,
        out_shape=jax.ShapeDtypeStruct(queries.shape, jnp.bfloat16),
        cost_estimate=pl.CostEstimate(
            flops=8 * pairs, bytes_accessed=8 * queries.size, transcendentals=pairs // HEAD_DIM
        ),
        compiler_params=pltpu.CompilerParams(vmem_limit_bytes=48 * 1024 * 1024),
    )(queries, keys, values, live.reshape(1, length))


def attend_back(queries, keys, values, grad_ctx, live, back_dtype):
    count, rows, width = queries.shape
    length = keys.shape[1]
    q_spec = pl.BlockSpec((1, rows, LANES), lambda i, h: (i, 0, h))
    k_spec = pl.BlockSpec((1, length, LANES), lambda i, h: (i, 0, h))
    pairs = count * rows * length * width
    return pl.pallas_call(
        attend_back_kernel,
        grid=(count, width // LANES),
        in_specs=[q_spec, k_spec, k_spec, q_spec, pl.BlockSpec((length, 1), lambda i, h: (0, 0))],
        out_specs=[q_spec, k_spec, k_spec],
        out_shape=[
            jax.ShapeDtypeStruct(queries.shape, jnp.float32),
            jax.ShapeDtypeStruct(keys.shape, back_dtype),
            jax.ShapeDtypeStruct(keys.shape, back_dtype),
        ],
        cost_estimate=pl.CostEstimate(
            flops=20 * pairs, bytes_accessed=20 * queries.size, transcendentals=pairs // HEAD_DIM
        ),
        compiler_params=pltpu.CompilerParams(vmem_limit_bytes=56 * 1024 * 1024),
    )(queries, keys, values, grad_ctx, live.reshape(length, 1))


def shift_by(step, ways):
    return [(i, (i + step) % ways) for i in range(ways)]


def spread(tokens):
    ways = lax.axis_size("seq")
    me = lax.axis_index("seq")
    each = tokens.shape[0] // ways
    parts = [lax.dynamic_slice_in_dim(tokens, me * each, each, 0)]
    for step in range(1, ways):
        target = lax.rem(me + step, ways)
        piece = lax.dynamic_slice_in_dim(tokens, target * each, each, 0)
        parts.append(lax.ppermute(piece, "seq", shift_by(step, ways)))
    return jnp.concatenate(parts, axis=1)


def unspread(tokens):
    ways = lax.axis_size("seq")
    me = lax.axis_index("seq")
    each, length, width = tokens.shape
    group = length // ways
    result = jnp.zeros((each * ways, group, width), tokens.dtype)
    for step in range(ways):
        piece = tokens[:, step * group : (step + 1) * group]
        if step:
            piece = lax.ppermute(piece, "seq", shift_by(-step, ways))
        source = lax.rem(me + step, ways)
        result = lax.dynamic_update_slice_in_dim(result, piece, source * each, 0)
    return result


def sum_over_seq(terms, axis):
    ways = lax.axis_size("seq")
    me = lax.axis_index("seq")
    size = terms.shape[axis] // ways
    total = lax.dynamic_slice_in_dim(terms, me * size, size, axis).astype(jnp.float32)
    for step in range(1, ways):
        target = lax.rem(me + step, ways)
        piece = lax.dynamic_slice_in_dim(terms, target * size, size, axis)
        total = total + lax.ppermute(piece, "seq", shift_by(step, ways)).astype(jnp.float32)
    return total


def body(
    images,
    cotangent,
    w_qkv,
    w_out,
    w_up,
    w_down,
    gains,
    biases,
    first_qkv,
    first_out,
    first_up,
    first_down,
    first_gains,
    first_biases,
    second_qkv,
    second_out,
    second_up,
    second_down,
    second_gains,
    second_biases,
):
    params = (w_qkv, w_out, w_up, w_down, gains, biases)
    firsts = (first_qkv, first_out, first_up, first_down, first_gains, first_biases)
    seconds = (second_qkv, second_out, second_up, second_down, second_gains, second_biases)
    count, group, width = images.shape
    ways = lax.axis_size("seq")
    blocks = lax.axis_size("dp")
    me = lax.axis_index("seq")
    pad_len = group * ways
    by_image = count % ways == 0
    rows_dp = w_qkv.shape[0]
    cols = w_out.shape[1]
    fold = w_up.shape[1] // cols
    own = gains.shape[1]
    small = jnp.concatenate([gains, biases], axis=0).astype(jnp.bfloat16).T
    lanes = -(-small.shape[1] // LANES) * LANES
    small = jnp.pad(small, ((0, rows_dp - own), (0, lanes - small.shape[1])))
    part_a = jnp.concatenate([w_qkv.astype(jnp.bfloat16), small], axis=1)
    wide_a = lax.all_gather(part_a, ("seq", "dp"), axis=0, tiled=True)
    part_b = jnp.concatenate(
        [
            w_out.astype(jnp.bfloat16),
            w_up.astype(jnp.bfloat16)
            .reshape(rows_dp, fold, cols)
            .transpose(1, 0, 2)
            .reshape(fold * rows_dp, cols),
            w_down.astype(jnp.bfloat16),
        ],
        axis=0,
    )
    part_b, wide_a = lax.optimization_barrier((part_b, wide_a))
    wide_b = lax.all_gather(part_b, ("seq", "dp"), axis=0, tiled=True)
    wide_a = wide_a.reshape(ways, width, part_a.shape[1])
    wide_qkv = jnp.concatenate([wide_a[k, :, : w_qkv.shape[1]] for k in range(ways)], axis=1)
    wide_small = (
        wide_a.reshape(ways, blocks, rows_dp, part_a.shape[1])[
            :, :, :own, w_qkv.shape[1] : w_qkv.shape[1] + 12
        ]
        .astype(jnp.float32)
        .transpose(3, 1, 0, 2)
        .reshape(12, width)
    )
    gain, bias = wide_small[:2], wide_small[2:]
    back_gain = gain
    wide_b = wide_b.reshape(ways, blocks, part_b.shape[0], cols)
    wide_out = wide_b[:, :, :rows_dp].transpose(1, 2, 0, 3).reshape(width, width)
    wide_up = (
        wide_b[:, :, rows_dp : (1 + fold) * rows_dp]
        .reshape(ways, blocks, fold, rows_dp, cols)
        .transpose(1, 3, 0, 2, 4)
        .reshape(width, fold * width)
    )
    wide_down = (
        wide_b[:, :, (1 + fold) * rows_dp :].transpose(1, 2, 0, 3).reshape(fold * width, width)
    )
    back_qkv, back_out, back_up, back_down = wide_qkv, wide_out, wide_up, wide_down
    spot = jnp.arange(group, dtype=jnp.int32)
    if by_image:
        images, cotangent = spread(images), spread(cotangent)
        token_live = jnp.concatenate(
            [lax.rem(me - k + ways, ways) * group + spot for k in range(ways)]
        ) < PATCH_TOK
        key_live = token_live
    else:
        token_live = me * group + spot < PATCH_TOK
        key_live = jnp.arange(pad_len, dtype=jnp.int32) < PATCH_TOK
    query_live = token_live
    key_live = key_live.astype(jnp.float32)
    rows = images.astype(jnp.float32)
    normed_a, inverse_a = normalize(rows)
    hidden_a = (normed_a * gain[0] + bias[0]).astype(jnp.bfloat16)
    mixed = jnp.einsum("icd,de->ice", hidden_a, wide_qkv, preferred_element_type=jnp.float32)
    queries = (mixed[..., :width] + bias[1]).astype(jnp.bfloat16)
    keys = mixed[..., width : 2 * width].astype(jnp.bfloat16)
    values = (mixed[..., 2 * width :] + bias[2]).astype(jnp.bfloat16)
    if by_image:
        keys_all, values_all = keys, values
    else:
        keys_all, values_all = (
            lax.all_gather(keys, "seq", axis=1, tiled=True),
            lax.all_gather(values, "seq", axis=1, tiled=True),
        )
    context = attend(queries, keys_all, values_all, key_live)
    resid = (
        rows
        + jnp.einsum("icd,de->ice", context, wide_out, preferred_element_type=jnp.float32)
        + bias[3]
    )
    normed_b, inverse_b = normalize(resid)
    hidden_b = (normed_b * gain[1] + bias[4]).astype(jnp.bfloat16)
    pre = jnp.einsum("icd,df->icf", hidden_b, wide_up, preferred_element_type=jnp.float32) + bias[
        6:
    ].reshape(-1)
    active = gelu_value(pre).astype(jnp.bfloat16)
    out_images = (
        resid
        + jnp.einsum("icf,fd->icd", active, wide_down, preferred_element_type=jnp.float32)
        + bias[5]
    ).astype(jnp.bfloat16)
    grad_y = cotangent.astype(jnp.float32) * query_live[None, :, None].astype(jnp.float32)
    grad_yb = grad_y.astype(jnp.bfloat16)
    g_down = jnp.einsum("icf,icd->fd", active, grad_yb, preferred_element_type=jnp.float32)
    grad_pre = jnp.einsum(
        "icd,fd->icf", grad_yb, back_down, preferred_element_type=jnp.float32
    ) * gelu_slope(pre)
    grad_preb = grad_pre.astype(jnp.bfloat16)
    g_up = jnp.einsum("icd,icf->df", hidden_b, grad_preb, preferred_element_type=jnp.float32)
    grad_hb = jnp.einsum("icf,df->icd", grad_preb, back_up, preferred_element_type=jnp.float32)
    grad_resid = grad_y + norm_back(grad_hb, normed_b, inverse_b, back_gain[1])
    grad_rb = grad_resid.astype(jnp.bfloat16)
    g_outw = jnp.einsum("icd,ice->de", context, grad_rb, preferred_element_type=jnp.float32)
    grad_ctx = jnp.einsum(
        "ice,de->icd", grad_rb, back_out, preferred_element_type=jnp.float32
    ).astype(jnp.bfloat16)
    grad_q, grad_k, grad_v = attend_back(
        queries,
        keys_all,
        values_all,
        grad_ctx,
        key_live,
        jnp.float32 if by_image else jnp.bfloat16,
    )
    if not by_image:
        grad_k, grad_v = (
            lax.psum_scatter(grad_k, "seq", scatter_dimension=1, tiled=True).astype(jnp.float32),
            lax.psum_scatter(grad_v, "seq", scatter_dimension=1, tiled=True).astype(jnp.float32),
        )
    grad_mixed = jnp.concatenate([grad_q, grad_k, grad_v], axis=-1).astype(jnp.bfloat16)
    g_qkv = jnp.einsum("icd,ice->de", hidden_a, grad_mixed, preferred_element_type=jnp.float32)
    grad_ha = jnp.einsum("ice,de->icd", grad_mixed, back_qkv, preferred_element_type=jnp.float32)
    grad_images = (grad_resid + norm_back(grad_ha, normed_a, inverse_a, back_gain[0])).astype(
        jnp.bfloat16
    )
    g_gains = jnp.stack(
        [jnp.sum(grad_ha * normed_a, axis=(0, 1)), jnp.sum(grad_hb * normed_b, axis=(0, 1))]
    )
    g_biases = jnp.concatenate(
        [
            jnp.stack(
                [
                    jnp.sum(grad_ha, axis=(0, 1)),
                    jnp.sum(grad_q, axis=(0, 1)),
                    jnp.sum(grad_v, axis=(0, 1)),
                    jnp.sum(grad_resid, axis=(0, 1)),
                    jnp.sum(grad_hb, axis=(0, 1)),
                    jnp.sum(grad_y, axis=(0, 1)),
                ]
            ),
            jnp.sum(grad_pre, axis=(0, 1)).reshape(-1, width),
        ],
        axis=0,
    )
    if by_image:
        out_images, grad_images = unspread(out_images), unspread(grad_images)
    send_a = jnp.concatenate(
        [
            g_outw.astype(jnp.bfloat16).reshape(blocks, rows_dp, width),
            g_up.astype(jnp.bfloat16)
            .reshape(blocks, rows_dp, ways, fold, cols)
            .transpose(0, 3, 1, 2, 4)
            .reshape(blocks, fold * rows_dp, width),
            g_down.astype(jnp.bfloat16).reshape(blocks, fold * rows_dp, width),
        ],
        axis=1,
    ).reshape(-1, width)
    part = lax.psum_scatter(send_a, "dp", scatter_dimension=0, tiled=True)
    total_a = sum_over_seq(part, 1)
    g_small = jnp.concatenate([g_gains, g_biases], axis=0).astype(jnp.bfloat16).T
    g_small = jnp.pad(g_small, ((0, 0), (0, lanes - g_small.shape[1])))
    send_b = jnp.concatenate([g_qkv.astype(jnp.bfloat16), g_small], axis=1)
    part, _ = lax.optimization_barrier((send_b, part))
    part = lax.psum_scatter(part, "dp", scatter_dimension=0, tiled=True)
    total_qkv = sum_over_seq(part[:, : g_qkv.shape[1]], 1)
    total_small = sum_over_seq(part[:, g_qkv.shape[1] :], 0)[:, :12].T
    totals = (
        total_qkv,
        total_a[:rows_dp],
        total_a[rows_dp : (1 + fold) * rows_dp]
        .reshape(fold, rows_dp, cols)
        .transpose(1, 0, 2)
        .reshape(rows_dp, fold * cols),
        total_a[(1 + fold) * rows_dp :],
        total_small[:2],
        total_small[2:],
    )
    updated = [
        adamw(param, grad, first, second)
        for param, grad, first, second in zip(params, totals, firsts, seconds)
    ]
    news = tuple((entry[0] for entry in updated))
    new_firsts = tuple((entry[1] for entry in updated))
    new_seconds = tuple((entry[2] for entry in updated))
    return (
        out_images,
        grad_images,
        totals[0],
        totals[1],
        totals[2],
        totals[3],
        totals[4],
        totals[5],
        news[0],
        news[1],
        news[2],
        news[3],
        news[4],
        news[5],
        new_firsts[0],
        new_firsts[1],
        new_firsts[2],
        new_firsts[3],
        new_firsts[4],
        new_firsts[5],
        new_seconds[0],
        new_seconds[1],
        new_seconds[2],
        new_seconds[3],
        new_seconds[4],
        new_seconds[5],
    )


def solution(mesh):
    return jax.shard_map(
        body,
        mesh=mesh,
        in_specs=(
            P("dp", "seq", None),
            P("dp", "seq", None),
            P("dp", "seq"),
            P("dp", "seq"),
            P("dp", "seq"),
            P("dp", "seq"),
            P(None, ("dp", "seq")),
            P(None, ("dp", "seq")),
            P("dp", "seq"),
            P("dp", "seq"),
            P("dp", "seq"),
            P("dp", "seq"),
            P(None, ("dp", "seq")),
            P(None, ("dp", "seq")),
            P("dp", "seq"),
            P("dp", "seq"),
            P("dp", "seq"),
            P("dp", "seq"),
            P(None, ("dp", "seq")),
            P(None, ("dp", "seq")),
        ),
        out_specs=(
            P("dp", "seq", None),
            P("dp", "seq", None),
            P("dp", "seq"),
            P("dp", "seq"),
            P("dp", "seq"),
            P("dp", "seq"),
            P(None, ("dp", "seq")),
            P(None, ("dp", "seq")),
            P("dp", "seq"),
            P("dp", "seq"),
            P("dp", "seq"),
            P("dp", "seq"),
            P(None, ("dp", "seq")),
            P(None, ("dp", "seq")),
            P("dp", "seq"),
            P("dp", "seq"),
            P("dp", "seq"),
            P("dp", "seq"),
            P(None, ("dp", "seq")),
            P(None, ("dp", "seq")),
            P("dp", "seq"),
            P("dp", "seq"),
            P("dp", "seq"),
            P("dp", "seq"),
            P(None, ("dp", "seq")),
            P(None, ("dp", "seq")),
        ),
        check_vma=False,
    )
```
